512 devices in a mesh: freq: 32 (over x, z_hi, core), skel: 16 (over z_lo, y).
Axes of the slice: x: 4, y: 4, z: 16 (z_hi: 4, z_lo: 4; z = z_hi * 4 + z_lo), core: 2. Of those that a mesh axis runs over, the one named last changes fastest.
Arguments:
- incident: bfloat16 [32, 32768, 128], P('freq', 'skel'), may hold values from -6 to 6
- compress: bfloat16 [32, 32768, 128], P('freq', 'skel'), may hold values from -0.125 to 0.125
- coupling: bfloat16 [32, 2, 2048, 2048], P('freq', None, None, 'skel'), may hold values from -0.125 to 0.125
- expand: bfloat16 [32, 32768, 128], P('freq', 'skel'), may hold values from -0.5 to 0.5
- box_list: int32 [32], replicated, may hold values from 0 to 31, each once
- spectrum: float32 [32], replicated, may hold values from 0.1 to 0.4
Outputs:
- pulse: bfloat16 [32768, 64, 256], P(('skel', 'freq'))
The draws below stay inside these ranges and needn't reach their ends.
Inputs may be any that keep to these rules, and one draw needn't show every extreme that they name: box_list names every box once.
All inputs are finite; a program needn't handle non-finite values.
Results may differ from the reference program's by a relative error of at most 0.007.
Values may be sent and summed in bfloat16 or wider, within the bound.
No kernel may reach another device: no remote copies, remote signals or barrier semaphores. Data moves between devices by JAX's collectives and lax.ppermute only.
A program may use at most 64 MiB of HBM per device.

```python
import math
import jax
import jax.numpy as jnp
from jax import lax

NB = 32768
BOX = 1024
R = 64
ANG = 64
NT = 2048
FREQ_LOW = 640
TWIN = 256
FREQS = 32
NBOX = 32
NS = 2048


def with_spikes(array, stream_key, source, target, shards_of, factor):
    owner, partner = [(jnp.arange(array.shape[dim]) // (array.shape[dim] // shards_of)).reshape([-1 if axis == dim else 1 for axis in range(array.ndim)]) for dim in (source, target)]
    chosen = jax.random.permutation(stream_key, shards_of)[partner]
    strong = (owner == chosen) | (owner == (partner + shards_of // 2) % shards_of)
    return jnp.where(strong, factor * array, array)


def steps_of(key, shape, pieces, smallest, largest):
    factor_of = 1.0
    for position, parts in pieces:
        draws = jax.random.uniform(jax.random.fold_in(jax.random.fold_in(key, 6), position), (parts,), jnp.float32, smallest / len(pieces), largest / len(pieces))
        factor_of = factor_of * jnp.repeat(jnp.exp(draws), shape[position] // parts).reshape((-1,) + (1,) * (len(shape) - 1 - position))
    return factor_of


def noise(stream_key, extent, width, reach, shards=(), kind=jnp.bfloat16):
    gain = steps_of(stream_key, extent, shards, -0.22, 0.18) if shards else 1.0
    result = jax.random.normal(stream_key, extent, jnp.float32) * width * gain
    return jnp.minimum(jnp.maximum(result, -reach), reach).astype(kind)


def gaussian_with(own_key, extent, scale, most, shards, heavy, held_as=jnp.bfloat16):
    entries = scale * jax.random.normal(own_key, extent, jnp.float32)
    if shards:
        entries = entries * steps_of(own_key, extent, shards, -0.22, 0.18)
    return jnp.clip(with_spikes(entries, jax.random.fold_in(own_key, 3), *heavy), -most, most).astype(held_as)


def setup_inputs(seed: int = 0) -> dict:
    key_of = jax.random.split(jax.random.key(seed), 7)
    incident = noise(key_of[0], (FREQS, NB, 2 * ANG), 1.0, 6.0, ((0, 32), (1, 16)))
    compress = noise(key_of[1], (FREQS, NB, 2 * R), (2 * BOX) ** -0.5, 0.125, ((0, 32), (1, 16)))
    coupling = gaussian_with(key_of[2], (FREQS, 2, NS, NS), (2 * NS) ** -0.5, 0.125, ((0, 32), (3, 16)), (3, 2, 16, 2.0))
    expand = noise(key_of[3], (FREQS, NB, 2 * R), (2 * R) ** -0.5, 0.5, ((0, 32), (1, 16)))
    box_list = jax.random.permutation(key_of[4], NBOX).astype(jnp.int32)
    spectrum = jnp.clip(jnp.exp(jax.random.uniform(key_of[5], (FREQS,), jnp.float32, math.log(0.1), math.log(0.4))), 0.1, 0.4)
    return {"incident": incident, "compress": compress, "coupling": coupling, "expand": expand, "box_list": box_list, "spectrum": spectrum}


def stack_complex(values):
    real_part = values[..., :ANG]
    imag_part = values[..., ANG:]
    top = jnp.concatenate([real_part, imag_part], axis=-1)
    bottom = jnp.concatenate([-imag_part, real_part], axis=-1)
    return jnp.concatenate([top, bottom], axis=-2)


def reference(incident, compress, coupling, expand, box_list, spectrum):
    def one_freq(operands):
        field, factors, matrix, expansion = operands
        product = jnp.einsum('kxr,kxa->kra', factors.reshape(NBOX, BOX, 2 * R).astype(jnp.float32),
                             field.reshape(NBOX, BOX, 2 * ANG).astype(jnp.float32))
        real_part = product[:, :R, :ANG] - product[:, R:, ANG:]
        imag_part = product[:, :R, ANG:] + product[:, R:, :ANG]
        compressed = jnp.concatenate([real_part, imag_part], axis=-1).astype(jnp.bfloat16).reshape(NS, 2 * ANG)
        first = jnp.dot(matrix[0], compressed, preferred_element_type=jnp.float32)
        second = jnp.dot(matrix[1], compressed, preferred_element_type=jnp.float32)
        coupled = jnp.concatenate([first[:, :ANG] - second[:, ANG:], first[:, ANG:] + second[:, :ANG]], axis=-1)
        owned = jnp.take(coupled.reshape(NBOX, R, 2 * ANG), box_list, axis=0).astype(jnp.bfloat16)
        stacked = stack_complex(owned)
        response = jnp.einsum('kxr,kra->kxa', expansion.reshape(NBOX, BOX, 2 * R).astype(jnp.float32),
                              stacked.astype(jnp.float32))
        return response.astype(jnp.bfloat16).reshape(NB, 2 * ANG)

    responses = lax.map(one_freq, (incident, compress, coupling, expand))
    freq_index = jnp.arange(FREQS, dtype=jnp.int32) + FREQ_LOW
    time_index = jnp.arange(TWIN, dtype=jnp.int32)
    phases = ((freq_index[:, None] * time_index[None, :]) % NT).astype(jnp.float32) * (2.0 * math.pi / NT)
    weights = spectrum[:, None]
    dft_table = jnp.stack([weights * jnp.cos(phases), -weights * jnp.sin(phases)]).astype(jnp.bfloat16)
    by_box = jnp.transpose(responses.reshape(FREQS, NBOX, BOX, 2, ANG), (1, 0, 2, 3, 4))

    def one_box(block):
        traces = jnp.einsum('fnca,cft->nat', block.astype(jnp.float32), dft_table.astype(jnp.float32))
        return traces.astype(jnp.bfloat16)

    pulse = lax.map(one_box, by_box)
    return pulse.reshape(NB, ANG, TWIN)
```

```python
import math

import jax
import jax.numpy as jnp
from jax import lax
from jax.sharding import PartitionSpec as P

BOX = 1024
NT = 2048
FREQ_LOW = 640
TWIN = 256


def time_table(spectrum):
    all_freqs = spectrum.shape[0]
    freq_index = jnp.arange(all_freqs, dtype=jnp.int32) + FREQ_LOW
    time_index = jnp.arange(TWIN, dtype=jnp.int32)
    phases = (freq_index[:, None] * time_index[None, :] % NT).astype(jnp.float32) * (
        2.0 * math.pi / NT
    )
    weights = spectrum[:, None]
    return jnp.stack([weights * jnp.cos(phases), -weights * jnp.sin(phases)]).astype(
        jnp.bfloat16
    )


def turned(values, angles):
    return jnp.concatenate([-values[..., angles:], values[..., :angles]], axis=-1)


def on_device(incident, compress, coupling, expand, box_list, spectrum, *, freqs, skels):
    local_rows, columns = incident.shape[1:]
    angles = columns // 2
    rank_cols = compress.shape[2]
    rank = rank_cols // 2
    boxes = local_rows // BOX
    product = jnp.einsum(
        "kxr,kxa->kra",
        compress.reshape(boxes, BOX, rank_cols),
        incident.reshape(boxes, BOX, columns),
        preferred_element_type=jnp.float32,
    )
    compressed = product[:, :rank] + turned(product[:, rank:], angles)
    compressed = compressed.astype(jnp.bfloat16).reshape(boxes * rank, columns)
    both = jnp.stack([compressed, turned(compressed, angles)])
    all_boxes = coupling.shape[2] // rank
    partial = jnp.einsum(
        "pmk,pka->ma", coupling[0], both, preferred_element_type=jnp.float32
    ).astype(jnp.bfloat16)
    picked = jnp.take(partial.reshape(all_boxes, rank * columns // 128, 128), box_list, axis=0)
    sent = picked.reshape(skels, boxes * rank, columns)
    parts = lax.all_to_all(sent, "skel", split_axis=0, concat_axis=0, tiled=True)
    owned = jnp.sum(parts.astype(jnp.float32), axis=0).astype(jnp.bfloat16)
    owned = owned.reshape(boxes, rank, columns)
    stacked = jnp.concatenate([owned, turned(owned, angles)], axis=1)
    response = jnp.einsum(
        "kxr,kra->kxa",
        expand.reshape(boxes, BOX, rank_cols),
        stacked,
        preferred_element_type=jnp.float32,
    ).astype(jnp.bfloat16)
    response = response.reshape(freqs, local_rows // freqs, columns)
    spaced = lax.all_to_all(response, "freq", split_axis=0, concat_axis=0, tiled=True)
    traces = jnp.einsum(
        "fnca,cft->nat",
        spaced.reshape(freqs, local_rows // freqs, 2, angles),
        time_table(spectrum),
        preferred_element_type=jnp.float32,
    )
    return traces.astype(jnp.bfloat16)


def solution(mesh):
    placed = (
        P("freq", "skel", None),
        P("freq", "skel", None),
        P("freq", None, None, "skel"),
        P("freq", "skel", None),
        P(),
        P(),
    )

    def body(*args):
        return on_device(*args, freqs=mesh.shape["freq"], skels=mesh.shape["skel"])

    return jax.shard_map(
        body,
        mesh=mesh,
        in_specs=placed,
        out_specs=P(("skel", "freq"), None, None),
        check_vma=False,
    )
```

```python
import functools
import math

import jax
import jax.numpy as jnp
from jax import lax
from jax.experimental import pallas as pl
from jax.experimental.pallas import tpu as pltpu
from jax.sharding import PartitionSpec as P

BOX = 1024
NT = 2048
FREQ_LOW = 640
TWIN = 256
CHUNK = 256
SMALL_GRANT = 12 << 20


def time_table(spectrum):
    all_freqs = spectrum.shape[0]
    freq_index = jnp.arange(all_freqs, dtype=jnp.int32) + FREQ_LOW
    time_index = jnp.arange(TWIN, dtype=jnp.int32)
    phases = (freq_index[:, None] * time_index[None, :] % NT).astype(jnp.float32) * (
        2.0 * math.pi / NT
    )
    weights = spectrum[:, None]
    return jnp.stack([weights * jnp.cos(phases), -weights * jnp.sin(phases)]).astype(
        jnp.bfloat16
    )


def turned(values):
    columns = values.shape[-1]
    swapped = pltpu.roll(values, columns // 2, 1)
    lane = lax.broadcasted_iota(jnp.int32, values.shape, 1)
    return jnp.where(lane < columns // 2, -swapped, swapped)


def front_kernel(boxes, rank, box_ref, compress_ref, incident_ref, coupling_ref, sent_ref, place_ref):
    all_boxes = box_ref.shape[0]
    for position in range(all_boxes):
        place_ref[box_ref[position]] = position
    plain, other = [], []
    for k in range(boxes):
        rows = pl.ds(k * BOX, BOX)
        product = lax.dot_general(
            compress_ref[rows, :],
            incident_ref[rows, :],
            (((0,), (0,)), ((), ())),
            preferred_element_type=jnp.float32,
        )
        compressed = product[:rank] + turned(product[rank:])
        compressed = compressed.astype(jnp.bfloat16).astype(jnp.float32)
        plain.append(compressed)
        other.append(turned(compressed))
    both = jnp.concatenate(plain + other, axis=0).astype(jnp.bfloat16)
    for start in range(0, all_boxes * rank, CHUNK):
        rows = pl.ds(start, CHUNK)
        matrix = jnp.concatenate([coupling_ref[0, rows, :], coupling_ref[1, rows, :]], axis=1)
        partial = jnp.dot(matrix, both, preferred_element_type=jnp.float32).astype(jnp.bfloat16)
        for part in range(CHUNK // rank):
            target = pl.multiple_of(place_ref[start // rank + part] * rank, rank)
            sent_ref[pl.ds(target, rank), :] = partial[part * rank : (part + 1) * rank]


def mid_kernel(boxes, rank, parts_ref, expand_ref, response_ref):
    total = parts_ref[0].astype(jnp.float32)
    for source in range(1, parts_ref.shape[0]):
        total = total + parts_ref[source].astype(jnp.float32)
    total = total.astype(jnp.bfloat16).astype(jnp.float32)
    for k in range(boxes):
        owned = total[k * rank : (k + 1) * rank]
        stacked = jnp.concatenate([owned, turned(owned)], axis=0).astype(jnp.bfloat16)
        for start in range(k * BOX, (k + 1) * BOX, CHUNK):
            rows = pl.ds(start, CHUNK)
            response_ref[rows, :] = jnp.dot(
                expand_ref[rows, :], stacked, preferred_element_type=jnp.float32
            ).astype(jnp.bfloat16)


def on_device(incident, compress, coupling, expand, box_list, spectrum, *, freqs, skels):
    local_rows, columns = incident.shape[1:]
    angles = columns // 2
    rank = compress.shape[2] // 2
    boxes = local_rows // BOX
    all_rows = coupling.shape[2]
    vmem = pl.BlockSpec(memory_space=pltpu.VMEM)
    sent = pl.pallas_call(
        functools.partial(front_kernel, boxes, rank),
        out_shape=jax.ShapeDtypeStruct((all_rows, columns), jnp.bfloat16),
        in_specs=[pl.BlockSpec(memory_space=pltpu.SMEM), vmem, vmem, vmem],
        out_specs=vmem,
        scratch_shapes=[pltpu.SMEM((all_rows // rank,), jnp.int32)],
        name="front",
    )(box_list, compress[0], incident[0], coupling[0])
    sent = sent.reshape(skels, all_rows // skels, columns)
    parts = lax.all_to_all(sent, "skel", split_axis=0, concat_axis=0, tiled=True)
    response = pl.pallas_call(
        functools.partial(mid_kernel, boxes, rank),
        out_shape=jax.ShapeDtypeStruct((local_rows, columns), jnp.bfloat16),
        in_specs=[vmem, vmem],
        out_specs=vmem,
        name="mid", compiler_params=pltpu.CompilerParams(vmem_limit_bytes=SMALL_GRANT),
    )(parts, expand[0])
    response = response.reshape(freqs, local_rows // freqs, columns)
    spaced = lax.all_to_all(response, "freq", split_axis=0, concat_axis=0, tiled=True)
    traces = jnp.einsum(
        "fnca,cft->nat",
        spaced.reshape(freqs, local_rows // freqs, 2, angles),
        time_table(spectrum),
        preferred_element_type=jnp.float32,
    )
    return traces.astype(jnp.bfloat16)


def solution(mesh):
    placed = (
        P("freq", "skel", None),
        P("freq", "skel", None),
        P("freq", None, None, "skel"),
        P("freq", "skel", None),
        P(),
        P(),
    )

    def body(*args):
        return on_device(*args, freqs=mesh.shape["freq"], skels=mesh.shape["skel"])

    return jax.shard_map(
        body,
        mesh=mesh,
        in_specs=placed,
        out_specs=P(("skel", "freq"), None, None),
        check_vma=False,
    )
```

```python
import functools
import math

import jax
import jax.numpy as jnp
from jax import lax
from jax.experimental import pallas as pl
from jax.experimental.pallas import tpu as pltpu
from jax.sharding import Mesh, PartitionSpec as P

BOX = 1024
NT = 2048
FREQ_LOW = 640
TWIN = 256
CHUNK = 256
SMALL_GRANT = 12 << 20


FREQ_AXES = ("x", "far", "core")
FREQ_SIZES = (4, 4, 2)
FREQ_WALK = ("far", "core", "x")
SKEL_AXES = ("near", "y")
SKEL_SIZES = (4, 4)
SKEL_WALK = ("y", "near")


def walked(sizes, axes, walk):
    members = []
    for place in range(math.prod(sizes)):
        at = {}
        for axis in reversed(walk):
            size = sizes[axes.index(axis)]
            at[axis] = place % size
            place //= size
        member = 0
        for axis, size in zip(axes, sizes):
            member = member * size + at[axis]
        members.append(member)
    return members


FREQ_ORDER = walked(FREQ_SIZES, FREQ_AXES, FREQ_WALK)
SKEL_ORDER = walked(SKEL_SIZES, SKEL_AXES, SKEL_WALK)


def in_walk(values):
    axes = [FREQ_AXES.index(axis) for axis in FREQ_WALK]
    return values.reshape(FREQ_SIZES).transpose(axes).reshape(-1)


def time_table(spectrum):
    all_freqs = spectrum.shape[0]
    spectrum = in_walk(spectrum)
    freq_index = in_walk(jnp.arange(all_freqs, dtype=jnp.int32)) + FREQ_LOW
    time_index = jnp.arange(TWIN, dtype=jnp.int32)
    phases = (freq_index[:, None] * time_index[None, :] % NT).astype(jnp.float32) * (
        2.0 * math.pi / NT
    )
    weights = spectrum[:, None]
    return jnp.stack([weights * jnp.cos(phases), -weights * jnp.sin(phases)]).astype(
        jnp.bfloat16
    )


def turned(values):
    columns = values.shape[-1]
    swapped = pltpu.roll(values, columns // 2, 1)
    lane = lax.broadcasted_iota(jnp.int32, values.shape, 1)
    return jnp.where(lane < columns // 2, -swapped, swapped)


def front_kernel(boxes, rank, box_ref, compress_ref, incident_ref, coupling_ref, sent_ref, place_ref):
    all_boxes = box_ref.shape[0]
    for position in range(all_boxes):
        place = SKEL_ORDER.index(position // boxes) * boxes + position % boxes
        place_ref[box_ref[position]] = place
    plain, other = [], []
    for k in range(boxes):
        rows = pl.ds(k * BOX, BOX)
        product = lax.dot_general(
            compress_ref[rows, :],
            incident_ref[rows, :],
            (((0,), (0,)), ((), ())),
            preferred_element_type=jnp.float32,
        )
        compressed = product[:rank] + turned(product[rank:])
        compressed = compressed.astype(jnp.bfloat16).astype(jnp.float32)
        plain.append(compressed)
        other.append(turned(compressed))
    both = jnp.concatenate(plain + other, axis=0).astype(jnp.bfloat16)
    for start in range(0, all_boxes * rank, CHUNK):
        rows = pl.ds(start, CHUNK)
        matrix = jnp.concatenate([coupling_ref[0, rows, :], coupling_ref[1, rows, :]], axis=1)
        partial = jnp.dot(matrix, both, preferred_element_type=jnp.float32).astype(jnp.bfloat16)
        for part in range(CHUNK // rank):
            target = pl.multiple_of(place_ref[start // rank + part] * rank, rank)
            sent_ref[pl.ds(target, rank), :] = partial[part * rank : (part + 1) * rank]


def mid_kernel(boxes, rank, parts_ref, expand_ref, response_ref):
    strip = response_ref.shape[1]
    total = parts_ref[0].astype(jnp.float32)
    for source in range(1, parts_ref.shape[0]):
        total = total + parts_ref[source].astype(jnp.float32)
    total = total.astype(jnp.bfloat16).astype(jnp.float32)
    for k in range(boxes):
        owned = total[k * rank : (k + 1) * rank]
        stacked = jnp.concatenate([owned, turned(owned)], axis=0).astype(jnp.bfloat16)
        for start in range(k * BOX, (k + 1) * BOX, CHUNK):
            rows = pl.ds(start, CHUNK)
            response = jnp.dot(
                expand_ref[rows, :], stacked, preferred_element_type=jnp.float32
            ).astype(jnp.bfloat16)
            for part in range(CHUNK // strip):
                place = FREQ_ORDER.index(start // strip + part)
                response_ref[place] = response[part * strip : (part + 1) * strip]


def on_device(incident, compress, coupling, expand, box_list, spectrum, *, freqs, skels):
    local_rows, columns = incident.shape[1:]
    angles = columns // 2
    rank = compress.shape[2] // 2
    boxes = local_rows // BOX
    all_rows = coupling.shape[2]
    vmem = pl.BlockSpec(memory_space=pltpu.VMEM)
    sent = pl.pallas_call(
        functools.partial(front_kernel, boxes, rank),
        out_shape=jax.ShapeDtypeStruct((all_rows, columns), jnp.bfloat16),
        in_specs=[pl.BlockSpec(memory_space=pltpu.SMEM), vmem, vmem, vmem],
        out_specs=vmem,
        scratch_shapes=[pltpu.SMEM((all_rows // rank,), jnp.int32)],
        name="front",
    )(box_list, compress[0], incident[0], coupling[0])
    sent = sent.reshape(skels, all_rows // skels, columns)
    parts = lax.all_to_all(sent, SKEL_WALK, split_axis=0, concat_axis=0, tiled=True)
    response = pl.pallas_call(
        functools.partial(mid_kernel, boxes, rank),
        out_shape=jax.ShapeDtypeStruct((freqs, local_rows // freqs, columns), jnp.bfloat16),
        in_specs=[vmem, vmem],
        out_specs=vmem,
        name="mid", compiler_params=pltpu.CompilerParams(vmem_limit_bytes=SMALL_GRANT),
    )(parts, expand[0])
    spaced = lax.all_to_all(response, FREQ_WALK, split_axis=0, concat_axis=0, tiled=True)
    traces = jnp.einsum(
        "fnca,cft->nat",
        spaced.reshape(freqs, local_rows // freqs, 2, angles),
        time_table(spectrum),
        preferred_element_type=jnp.float32,
    )
    return traces.astype(jnp.bfloat16)


def solution(mesh):
    chips = Mesh(mesh.devices.reshape(FREQ_SIZES + SKEL_SIZES), FREQ_AXES + SKEL_AXES)
    placed = (
        P(FREQ_AXES, SKEL_AXES, None),
        P(FREQ_AXES, SKEL_AXES, None),
        P(FREQ_AXES, None, None, SKEL_AXES),
        P(FREQ_AXES, SKEL_AXES, None),
        P(),
        P(),
    )

    def body(*args):
        return on_device(*args, freqs=mesh.shape["freq"], skels=mesh.shape["skel"])

    return jax.shard_map(
        body,
        mesh=chips,
        in_specs=placed,
        out_specs=P(SKEL_AXES + FREQ_AXES, None, None),
        check_vma=False,
    )
```

```python
import functools
import math

import jax
import jax.numpy as jnp
from jax import lax
from jax.experimental import pallas as pl
from jax.experimental.pallas import tpu as pltpu
from jax.sharding import Mesh, PartitionSpec as P

BOX = 1024
NT = 2048
FREQ_LOW = 640
TWIN = 256
CHUNK = 256
SMALL_GRANT = 12 << 20


FREQ_AXES = ("x", "far", "core")
FREQ_SIZES = (4, 4, 2)
FREQ_WALK = ("far", "core", "x")
SKEL_AXES = ("near", "y")
SKEL_SIZES = (4, 4)
SKEL_WALK = ("y", "near")


def walked(sizes, axes, walk):
    members = []
    for place in range(math.prod(sizes)):
        at = {}
        for axis in reversed(walk):
            size = sizes[axes.index(axis)]
            at[axis] = place % size
            place //= size
        member = 0
        for axis, size in zip(axes, sizes):
            member = member * size + at[axis]
        members.append(member)
    return members


FREQ_ORDER = walked(FREQ_SIZES, FREQ_AXES, FREQ_WALK)
SKEL_ORDER = walked(SKEL_SIZES, SKEL_AXES, SKEL_WALK)


def in_walk(values):
    axes = [FREQ_AXES.index(axis) for axis in FREQ_WALK]
    return values.reshape(FREQ_SIZES).transpose(axes).reshape(-1)


def time_table(spectrum):
    all_freqs = spectrum.shape[0]
    spectrum = in_walk(spectrum)
    freq_index = in_walk(jnp.arange(all_freqs, dtype=jnp.int32)) + FREQ_LOW
    time_index = jnp.arange(TWIN, dtype=jnp.int32)
    phases = (freq_index[:, None] * time_index[None, :] % NT).astype(jnp.float32) * (
        2.0 * math.pi / NT
    )
    weights = spectrum[:, None]
    return jnp.stack([weights * jnp.cos(phases), -weights * jnp.sin(phases)]).astype(
        jnp.bfloat16
    )


def turned(values):
    columns = values.shape[-1]
    swapped = pltpu.roll(values, columns // 2, 1)
    lane = lax.broadcasted_iota(jnp.int32, values.shape, 1)
    return jnp.where(lane < columns // 2, -swapped, swapped)


def front_kernel(boxes, rank, box_ref, compress_ref, incident_ref, coupling_ref, sent_ref, place_ref):
    all_boxes = box_ref.shape[0]
    for position in range(all_boxes):
        place = SKEL_ORDER.index(position // boxes) * boxes + position % boxes
        place_ref[box_ref[position]] = place
    plain, other = [], []
    for k in range(boxes):
        rows = pl.ds(k * BOX, BOX)
        product = lax.dot_general(
            compress_ref[rows, :],
            incident_ref[rows, :],
            (((0,), (0,)), ((), ())),
            preferred_element_type=jnp.float32,
        )
        compressed = product[:rank] + turned(product[rank:])
        compressed = compressed.astype(jnp.bfloat16).astype(jnp.float32)
        plain.append(compressed)
        other.append(turned(compressed))
    both = jnp.concatenate(plain + other, axis=0).astype(jnp.bfloat16)
    for start in range(0, all_boxes * rank, CHUNK):
        rows = pl.ds(start, CHUNK)
        matrix = jnp.concatenate([coupling_ref[0, rows, :], coupling_ref[1, rows, :]], axis=1)
        partial = jnp.dot(matrix, both, preferred_element_type=jnp.float32).astype(jnp.bfloat16)
        for part in range(CHUNK // rank):
            target = pl.multiple_of(place_ref[start // rank + part] * rank, rank)
            sent_ref[pl.ds(target, rank), :] = partial[part * rank : (part + 1) * rank]


def mid_kernel(boxes, rank, parts_ref, expand_ref, response_ref):
    strip = response_ref.shape[1]
    total = parts_ref[0].astype(jnp.float32)
    for source in range(1, parts_ref.shape[0]):
        total = total + parts_ref[source].astype(jnp.float32)
    total = total.astype(jnp.bfloat16).astype(jnp.float32)
    for k in range(boxes):
        owned = total[k * rank : (k + 1) * rank]
        stacked = jnp.concatenate([owned, turned(owned)], axis=0).astype(jnp.bfloat16)
        for start in range(k * BOX, (k + 1) * BOX, CHUNK):
            rows = pl.ds(start, CHUNK)
            response = jnp.dot(
                expand_ref[rows, :], stacked, preferred_element_type=jnp.float32
            ).astype(jnp.bfloat16)
            for part in range(CHUNK // strip):
                place = FREQ_ORDER.index(start // strip + part)
                response_ref[place] = response[part * strip : (part + 1) * strip]


def on_device(incident, compress, coupling, expand, box_list, spectrum, *, freqs, skels):
    local_rows, columns = incident.shape[1:]
    angles = columns // 2
    rank = compress.shape[2] // 2
    boxes = local_rows // BOX
    all_rows = coupling.shape[2]
    vmem = pl.BlockSpec(memory_space=pltpu.VMEM)
    sent = pl.pallas_call(
        functools.partial(front_kernel, boxes, rank),
        out_shape=jax.ShapeDtypeStruct((all_rows, columns), jnp.bfloat16),
        in_specs=[pl.BlockSpec(memory_space=pltpu.SMEM), vmem, vmem, vmem],
        out_specs=vmem,
        scratch_shapes=[pltpu.SMEM((all_rows // rank,), jnp.int32)],
        compiler_params=pltpu.CompilerParams(vmem_limit_bytes=56 << 20),
        name="front",
    )(box_list, compress[0], incident[0], coupling[0])
    sent = sent.reshape(skels, all_rows // skels, columns)
    parts = lax.all_to_all(sent, SKEL_WALK, split_axis=0, concat_axis=0, tiled=True)
    response = pl.pallas_call(
        functools.partial(mid_kernel, boxes, rank),
        out_shape=jax.ShapeDtypeStruct((freqs, local_rows // freqs, columns), jnp.bfloat16),
        in_specs=[vmem, vmem],
        out_specs=vmem,
        name="mid", compiler_params=pltpu.CompilerParams(vmem_limit_bytes=SMALL_GRANT),
    )(parts, expand[0])
    spaced = lax.all_to_all(response, FREQ_WALK, split_axis=0, concat_axis=0, tiled=True)
    traces = jnp.einsum(
        "fnca,cft->nat",
        spaced.reshape(freqs, local_rows // freqs, 2, angles),
        time_table(spectrum),
        preferred_element_type=jnp.float32,
    )
    return traces.astype(jnp.bfloat16)


def solution(mesh):
    chips = Mesh(mesh.devices.reshape(FREQ_SIZES + SKEL_SIZES), FREQ_AXES + SKEL_AXES)
    placed = (
        P(FREQ_AXES, SKEL_AXES, None),
        P(FREQ_AXES, SKEL_AXES, None),
        P(FREQ_AXES, None, None, SKEL_AXES),
        P(FREQ_AXES, SKEL_AXES, None),
        P(),
        P(),
    )

    def body(*args):
        return on_device(*args, freqs=mesh.shape["freq"], skels=mesh.shape["skel"])

    return jax.shard_map(
        body,
        mesh=chips,
        in_specs=placed,
        out_specs=P(SKEL_AXES + FREQ_AXES, None, None),
        check_vma=False,
    )
```
